32 devices in a mesh: section: 2 (over core), ctx: 4 (over y, x), wt: 4 (over z).
Axes of the slice: x: 2, y: 2, z: 4, core: 2. Of those that a mesh axis runs over, the one named last changes fastest.
Arguments:
- inputs: bfloat16 [2, 1024, 576], P(None, ('ctx', 'wt')), may hold values from -6 to 6
- doc_start: int32 [2, 1024], replicated, may hold values from 0 to 1791, as said below
- attn_gain: float32 [2, 576], P('section'), may hold values from 0.25 to 1.75
- w_q: bfloat16 [2, 576, 576], P('section', 'wt'), may hold values from -0.25 to 0.25
- key_projection: bfloat16 [2, 576, 192], P('section', 'wt'), may hold values from -0.25 to 0.25
- value_projection: bfloat16 [2, 576, 192], P('section', 'wt'), may hold values from -0.25 to 0.25
- w_o: bfloat16 [2, 576, 576], P('section', 'wt'), may hold values from -1.5 to 1.5
- mlp_gain: float32 [2, 576], P('section'), may hold values from 0.25 to 1.75
- w_gate: bfloat16 [2, 576, 1536], P('section', None, 'wt'), may hold values from -0.25 to 0.25
- w_up: bfloat16 [2, 576, 1536], P('section', None, 'wt'), may hold values from -0.25 to 0.25
- w_down: bfloat16 [2, 1536, 576], P('section', 'wt'), may hold values from -0.15625 to 0.15625
- cotangent: float32 [2, 1024, 576], P(None, ('ctx', 'wt')), may hold values from -6 to 6
Outputs:
- acts: bfloat16 [2, 2, 1024, 576], P('section', None, ('ctx', 'wt'))
- dacts: bfloat16 [2, 2, 1024, 576], P('section', None, ('ctx', 'wt'))
- grad_attn_gain: float32 [2, 576], P('section', 'wt')
- grad_w_q: float32 [2, 576, 576], P('section', 'wt')
- grad_w_k: float32 [2, 576, 192], P('section', 'wt')
- grad_w_v: float32 [2, 576, 192], P('section', 'wt')
- grad_w_o: float32 [2, 576, 576], P('section', 'wt')
- grad_mlp_gain: float32 [2, 576], P('section', 'wt')
- grad_w_gate: float32 [2, 576, 1536], P('section', None, 'wt')
- grad_w_up: float32 [2, 576, 1536], P('section', None, 'wt')
- grad_w_down: float32 [2, 1536, 576], P('section', 'wt')
The draws below stay inside these ranges and needn't reach their ends.
Inputs may be any that keep to these rules, and one draw needn't show every extreme that they name: `doc_start`: doc_start_i is the first position of token i's document in the sequence of 2048 tokens: never above i, never falling along the sequence, equal within a document; three documents, the last beginning at position 1791.
All inputs are finite; a program needn't handle non-finite values.
Results may differ from the reference program's by a relative error of at most 0.028.
Values may be sent and summed in bfloat16 or wider, within the bound.
A program may use at most 128 MiB of HBM per device.

```python
import math
import jax
import jax.numpy as jnp
from jax import lax

MODEL_DIMENSION = 576
QUERY_HEAD_COUNT = 9
KEY_VALUE_HEADS = 3
HEAD_DIMENSION = 64
FF = 1536
M = 2
TOK_MB = 1024


def draw_doc_start(key, part):
    running_sum = M * TOK_MB
    second_bound = running_sum - running_sum // 8 - 1
    first_bound = jax.random.randint(key, (), running_sum // 8, second_bound)
    positions = jnp.arange(running_sum, dtype=jnp.int32)
    starts = jnp.where(positions >= second_bound, second_bound, jnp.where(positions >= first_bound, first_bound, 0))
    return starts.reshape(M, TOK_MB).astype(jnp.int32)


def steps_of(key, shape, pieces, low, top_value):
    def one(position, blocks):
        draws = jax.random.uniform(jax.random.fold_in(jax.random.fold_in(key, 6), position), (blocks,), jnp.float32, low / len(pieces), top_value / len(pieces))
        return jnp.repeat(jnp.exp(draws), shape[position] // blocks).reshape((-1,) + (1,) * (len(shape) - position - 1))

    gain = one(*pieces[0])
    for cut in pieces[1:]:
        gain = gain * one(*cut)
    return gain


def normal_values(rng, extent, deviation, most, shards=(), kind=jnp.bfloat16):
    gain = steps_of(rng, extent, shards, -0.22, 0.18) if shards else 1.0
    drawn = jax.random.normal(rng, extent, jnp.float32) * deviation * gain
    return jnp.minimum(jnp.maximum(drawn, -most), most).astype(kind)


def setup_inputs(seed: int = 0) -> dict:
    key_of = jax.random.split(jax.random.key(seed), 13)
    inputs = normal_values(key_of[0], (M, TOK_MB, MODEL_DIMENSION), 1.0, 6.0, ((1, 16),))
    doc_start = draw_doc_start(jax.random.fold_in(key_of[12], 71), 0)
    attn_gain = jnp.clip(1.0 + 0.15 * jax.random.normal(key_of[2], (2, MODEL_DIMENSION), jnp.float32), 0.25, 1.75)
    w_q = normal_values(key_of[3], (2, MODEL_DIMENSION, MODEL_DIMENSION), MODEL_DIMENSION ** -0.5, 0.25, ((0, 2), (1, 4)))
    key_projection = normal_values(key_of[4], (2, MODEL_DIMENSION, KEY_VALUE_HEADS * HEAD_DIMENSION), MODEL_DIMENSION ** -0.5, 0.25, ((0, 2), (1, 4)))
    value_projection = normal_values(key_of[5], (2, MODEL_DIMENSION, KEY_VALUE_HEADS * HEAD_DIMENSION), MODEL_DIMENSION ** -0.5, 0.25, ((0, 2), (1, 4)))
    w_o = normal_values(key_of[6], (2, MODEL_DIMENSION, MODEL_DIMENSION), (MODEL_DIMENSION // 32) ** -0.5, 1.5, ((0, 2), (1, 4)))
    mlp_gain = jnp.clip(1.0 + 0.15 * jax.random.normal(key_of[7], (2, MODEL_DIMENSION), jnp.float32), 0.25, 1.75)
    w_gate = normal_values(key_of[8], (2, MODEL_DIMENSION, FF), MODEL_DIMENSION ** -0.5, 0.25, ((0, 2), (2, 4)))
    w_up = normal_values(key_of[9], (2, MODEL_DIMENSION, FF), MODEL_DIMENSION ** -0.5, 0.25, ((0, 2), (2, 4)))
    w_down = normal_values(key_of[10], (2, FF, MODEL_DIMENSION), FF ** -0.5, 0.15625, ((0, 2), (1, 4)))
    cotangent = normal_values(key_of[11], (M, TOK_MB, MODEL_DIMENSION), 1.0, 6.0, ((1, 16),), jnp.float32)
    return {"inputs": inputs, "doc_start": doc_start, "attn_gain": attn_gain, "w_q": w_q, "key_projection": key_projection, "value_projection": value_projection, "w_o": w_o, "mlp_gain": mlp_gain, "w_gate": w_gate, "w_up": w_up, "w_down": w_down, "cotangent": cotangent}


EPSILON = 1e-05
THETA = 100000.0
MASKED_FLOOR = -1e+30

def rounded(value_matrix):
    return lax.optimization_barrier(value_matrix.astype(jnp.bfloat16)).astype(jnp.float32)

def rope_tables(rotary):
    half_size = HEAD_DIMENSION // 2
    inverse = 1.0 / THETA ** (jnp.arange(half_size).astype(jnp.float32) * 2.0 / HEAD_DIMENSION)
    angles = rotary[:, None] * inverse[None, :]
    return (jnp.concatenate([jnp.cos(angles), jnp.cos(angles)], -1), jnp.concatenate([jnp.sin(angles), jnp.sin(angles)], -1))

def apply_rotation(value_matrix, cosine_values, sine_values):
    half_size = value_matrix.shape[-1] // 2
    turned = jnp.concatenate([-value_matrix[..., half_size:], value_matrix[..., :half_size]], -1)
    return value_matrix * cosine_values[:, None, :] + turned * sine_values[:, None, :]

def reverse_rotation(grads, cosine_values, sine_values):
    half_size = grads.shape[-1] // 2
    scaled = grads * sine_values[:, None, :]
    turned = jnp.concatenate([scaled[..., half_size:], -scaled[..., :half_size]], -1)
    return grads * cosine_values[:, None, :] + turned

def row_product(left_matrix, right_matrix):
    return lax.dot_general(left_matrix, right_matrix, (((0,), (0,)), ((), ())), preferred_element_type=jnp.float32)

def back_product(left_matrix, right_matrix):
    return lax.dot_general(left_matrix, right_matrix, (((1,), (1,)), ((), ())), preferred_element_type=jnp.float32)

def block_scores(rows_of_queries, key_rows, lower_limit, doc_flat):
    tally_count = rows_of_queries.shape[0]
    span = key_rows.shape[0]
    heads_of_queries = rows_of_queries.astype(jnp.float32).reshape(tally_count, KEY_VALUE_HEADS, QUERY_HEAD_COUNT // KEY_VALUE_HEADS, HEAD_DIMENSION)
    scores = jnp.einsum('qhge,khe->hgqk', heads_of_queries, key_rows.astype(jnp.float32)) * 0.125
    query_pos = lower_limit + jnp.arange(tally_count, dtype=jnp.int32)
    key_pos = jnp.arange(span, dtype=jnp.int32)
    query_doc = doc_flat[lower_limit:lower_limit + tally_count]
    allowed = (key_pos[None, :] <= query_pos[:, None]) & (key_pos[None, :] >= query_doc[:, None])
    return jnp.where(allowed[None, None], scores, MASKED_FLOOR)

def layer_forward(section_in, doc_flat, cosine_values, sine_values, params):
    attn_gain, w_q, key_projection, value_projection, w_o, mlp_gain, w_gate, w_up, w_down = params
    running_sum = section_in.shape[0]
    hidden = section_in.astype(jnp.float32)
    inverse1 = lax.rsqrt(lax.optimization_barrier(jnp.mean(hidden * hidden, -1, keepdims=True)) + EPSILON)
    normed1 = hidden * inverse1
    attention_input = (normed1 * attn_gain).astype(jnp.bfloat16)
    query_matrix = apply_rotation(jnp.dot(attention_input, w_q, preferred_element_type=jnp.float32).reshape(running_sum, QUERY_HEAD_COUNT, HEAD_DIMENSION), cosine_values, sine_values).astype(jnp.bfloat16)
    key_matrix = apply_rotation(jnp.dot(attention_input, key_projection, preferred_element_type=jnp.float32).reshape(running_sum, KEY_VALUE_HEADS, HEAD_DIMENSION), cosine_values, sine_values).astype(jnp.bfloat16)
    value_matrix = jnp.dot(attention_input, value_projection, preferred_element_type=jnp.float32).astype(jnp.bfloat16).reshape(running_sum, KEY_VALUE_HEADS, HEAD_DIMENSION)
    rows_per_block = math.gcd(running_sum, 512)
    mixed_parts = []
    log_parts = []
    for block_index in range(running_sum // rows_per_block):
        lower_limit = block_index * rows_per_block
        upper_limit = lower_limit + rows_per_block
        scores = block_scores(query_matrix[lower_limit:upper_limit], key_matrix[:upper_limit], lower_limit, doc_flat)
        row_top = lax.optimization_barrier(jnp.max(scores, -1))
        weights = jnp.exp(scores - row_top[..., None])
        summed = lax.optimization_barrier(jnp.sum(weights, -1))
        accumulated = jnp.einsum('hgqk,khe->hgqe', rounded(weights), value_matrix[:upper_limit].astype(jnp.float32))
        mixed_parts.append((accumulated / summed[..., None]).transpose(2, 0, 1, 3).reshape(rows_per_block, QUERY_HEAD_COUNT * HEAD_DIMENSION))
        log_parts.append(row_top + jnp.log(summed))
    blended_output = jnp.concatenate(mixed_parts, 0).astype(jnp.bfloat16)
    log_total = jnp.concatenate(log_parts, -1)
    residual = hidden + jnp.dot(blended_output, w_o, preferred_element_type=jnp.float32)
    inverse2 = lax.rsqrt(lax.optimization_barrier(jnp.mean(residual * residual, -1, keepdims=True)) + EPSILON)
    normed2 = residual * inverse2
    mlp_in = (normed2 * mlp_gain).astype(jnp.bfloat16)
    gate_pre = jnp.dot(mlp_in, w_gate, preferred_element_type=jnp.float32)
    up_pre = jnp.dot(mlp_in, w_up, preferred_element_type=jnp.float32)
    activated = (gate_pre * jax.nn.sigmoid(gate_pre) * up_pre).astype(jnp.bfloat16)
    result = (residual + jnp.dot(activated, w_down, preferred_element_type=jnp.float32)).astype(jnp.bfloat16)
    saved_state = (normed1, inverse1, attention_input, query_matrix, key_matrix, value_matrix, blended_output, log_total, normed2, inverse2, mlp_in, gate_pre, up_pre, activated)
    return (result, saved_state)

def attention_backward(query_matrix, key_matrix, value_matrix, blended_output, log_total, attention_gradient, doc_flat):
    running_sum = query_matrix.shape[0]
    query_groups = QUERY_HEAD_COUNT // KEY_VALUE_HEADS
    delta_per_row = lax.optimization_barrier(jnp.sum((attention_gradient.astype(jnp.float32) * blended_output.astype(jnp.float32)).reshape(running_sum, KEY_VALUE_HEADS, query_groups, HEAD_DIMENSION), -1))
    key_gradient_sum = jnp.zeros((running_sum, KEY_VALUE_HEADS, HEAD_DIMENSION), jnp.float32)
    value_gradient_sum = jnp.zeros((running_sum, KEY_VALUE_HEADS, HEAD_DIMENSION), jnp.float32)
    query_parts = []
    rows_per_block = math.gcd(running_sum, 512)
    for block_index in range(running_sum // rows_per_block):
        lower_limit = block_index * rows_per_block
        upper_limit = lower_limit + rows_per_block
        scores = block_scores(query_matrix[lower_limit:upper_limit], key_matrix[:upper_limit], lower_limit, doc_flat)
        probabilities = jnp.exp(scores - log_total[:, :, lower_limit:upper_limit][..., None])
        head_gradients = attention_gradient[lower_limit:upper_limit].astype(jnp.float32).reshape(rows_per_block, KEY_VALUE_HEADS, query_groups, HEAD_DIMENSION)
        heads_of_queries = query_matrix[lower_limit:upper_limit].astype(jnp.float32).reshape(rows_per_block, KEY_VALUE_HEADS, query_groups, HEAD_DIMENSION)
        value_gradient_sum = value_gradient_sum.at[:upper_limit].add(jnp.einsum('hgqk,qhge->khe', rounded(probabilities), head_gradients))
        grad_probs = jnp.einsum('qhge,khe->hgqk', head_gradients, value_matrix[:upper_limit].astype(jnp.float32))
        block_delta = delta_per_row[lower_limit:upper_limit].transpose(1, 2, 0)
        grad_scores = rounded(probabilities * (grad_probs - block_delta[..., None]))
        query_parts.append(jnp.einsum('hgqk,khe->qhge', grad_scores, key_matrix[:upper_limit].astype(jnp.float32)) * 0.125)
        key_gradient_sum = key_gradient_sum.at[:upper_limit].add(jnp.einsum('hgqk,qhge->khe', grad_scores, heads_of_queries) * 0.125)
    grad_query = jnp.concatenate(query_parts, 0).reshape(running_sum, QUERY_HEAD_COUNT, HEAD_DIMENSION)
    return (grad_query, key_gradient_sum, value_gradient_sum)

def layer_backward(saved_state, upstream, doc_flat, cosine_values, sine_values, params):
    attn_gain, w_q, key_projection, value_projection, w_o, mlp_gain, w_gate, w_up, w_down = params
    normed1, inverse1, attention_input, query_matrix, key_matrix, value_matrix, blended_output, log_total, normed2, inverse2, mlp_in, gate_pre, up_pre, activated = saved_state
    running_sum = upstream.shape[0]
    out_grad = upstream.astype(jnp.bfloat16)
    grad_down = row_product(activated, out_grad)
    grad_activated = back_product(out_grad, w_down)
    sigmoid_gate = jax.nn.sigmoid(gate_pre)
    grad_gate_rows = (grad_activated * up_pre * sigmoid_gate * (1.0 + gate_pre * (1.0 - sigmoid_gate))).astype(jnp.bfloat16)
    grad_up_rows = (grad_activated * gate_pre * sigmoid_gate).astype(jnp.bfloat16)
    grad_gate = row_product(mlp_in, grad_gate_rows)
    grad_up = row_product(mlp_in, grad_up_rows)
    grad_mlp_in = back_product(grad_gate_rows, w_gate) + back_product(grad_up_rows, w_up)
    grad_mlp_gain = lax.optimization_barrier(jnp.sum(grad_mlp_in * normed2, 0))
    scaled2 = grad_mlp_in * mlp_gain
    grad_residual = upstream + inverse2 * (scaled2 - normed2 * lax.optimization_barrier(jnp.mean(scaled2 * normed2, -1, keepdims=True)))
    residual_grad = grad_residual.astype(jnp.bfloat16)
    grad_out = row_product(blended_output, residual_grad)
    attention_gradient = back_product(residual_grad, w_o).astype(jnp.bfloat16)
    grad_query, key_gradient_sum, value_gradient_sum = attention_backward(query_matrix, key_matrix, value_matrix, blended_output, log_total, attention_gradient, doc_flat)
    grad_queries = reverse_rotation(grad_query, cosine_values, sine_values).astype(jnp.bfloat16).reshape(running_sum, QUERY_HEAD_COUNT * HEAD_DIMENSION)
    key_gradients = reverse_rotation(key_gradient_sum, cosine_values, sine_values).astype(jnp.bfloat16).reshape(running_sum, KEY_VALUE_HEADS * HEAD_DIMENSION)
    value_gradients = value_gradient_sum.astype(jnp.bfloat16).reshape(running_sum, KEY_VALUE_HEADS * HEAD_DIMENSION)
    grad_query_w = row_product(attention_input, grad_queries)
    grad_key_w = row_product(attention_input, key_gradients)
    grad_value_w = row_product(attention_input, value_gradients)
    grad_attn_in = back_product(grad_queries, w_q) + back_product(key_gradients, key_projection) + back_product(value_gradients, value_projection)
    grad_attn_gain = lax.optimization_barrier(jnp.sum(grad_attn_in * normed1, 0))
    scaled1 = grad_attn_in * attn_gain
    grad_input = (grad_residual + inverse1 * (scaled1 - normed1 * lax.optimization_barrier(jnp.mean(scaled1 * normed1, -1, keepdims=True)))).astype(jnp.bfloat16)
    return (grad_input, (grad_attn_gain, grad_query_w, grad_key_w, grad_value_w, grad_out, grad_mlp_gain, grad_gate, grad_up, grad_down))

def reference(inputs, doc_start, attn_gain, w_q, key_projection, value_projection, w_o, mlp_gain, w_gate, w_up, w_down, cotangent):
    running_sum = M * TOK_MB
    doc_flat = doc_start.reshape(running_sum).astype(jnp.int32)
    rotary = (jnp.arange(running_sum, dtype=jnp.int32) - doc_flat).astype(jnp.float32)
    cosine_values, sine_values = rope_tables(rotary)
    first_params = tuple((item[0] for item in (attn_gain, w_q, key_projection, value_projection, w_o, mlp_gain, w_gate, w_up, w_down)))
    second_params = tuple((item[1] for item in (attn_gain, w_q, key_projection, value_projection, w_o, mlp_gain, w_gate, w_up, w_down)))
    first_out, first_saved = layer_forward(inputs.reshape(running_sum, MODEL_DIMENSION), doc_flat, cosine_values, sine_values, first_params)
    second_out, second_saved = layer_forward(first_out, doc_flat, cosine_values, sine_values, second_params)
    second_grad, second_grads = layer_backward(second_saved, cotangent.reshape(running_sum, MODEL_DIMENSION), doc_flat, cosine_values, sine_values, second_params)
    first_grad, first_grads = layer_backward(first_saved, second_grad.astype(jnp.float32), doc_flat, cosine_values, sine_values, first_params)
    acts = jnp.stack([first_out, second_out]).reshape(2, M, TOK_MB, MODEL_DIMENSION)
    dacts = jnp.stack([first_grad, second_grad]).reshape(2, M, TOK_MB, MODEL_DIMENSION)
    stacked = [jnp.stack([first_item, second_item]) for first_item, second_item in zip(first_grads, second_grads)]
    return (acts, dacts, stacked[0], stacked[1], stacked[2], stacked[3], stacked[4], stacked[5], stacked[6], stacked[7], stacked[8])
```

```python
import functools

import jax
import jax.numpy as jnp
from jax import lax
from jax.experimental import pallas as pl
from jax.experimental.pallas import tpu as pltpu
from jax.sharding import PartitionSpec as P

HEADS = 9
KV = 3
GROUP = HEADS // KV
HD = 64
KVW = KV * HD
EPS = 1e-05
THETA = 100000.0
FLOOR = -1e30
BF = jnp.bfloat16
F32 = jnp.float32
VMEM_LIMIT = 60 * 1024 * 1024
MESH = pl.DeviceIdType.MESH

IDS = {}


def group_of(axes, sizes):
    count = 1
    for axis in axes:
        count *= sizes[axis]
    return count


def my_index(axes, sizes):
    index = 0
    for axis in axes:
        index = index * sizes[axis] + lax.axis_index(axis)
    return index


def device_at(axes, index, sizes):
    where = {}
    for axis in reversed(axes):
        where[axis] = lax.rem(index, sizes[axis])
        index = lax.div(index, sizes[axis])
    return where


def comm_kernel(plan, sizes, n_in, *refs):
    n_ops = len(plan)
    ins = refs[:n_in]
    outs = refs[n_in : n_in + n_ops]
    sems = refs[n_in + n_ops :]
    section = lax.axis_index("section")
    partner = {"section": 1 - section}
    groups = []
    swaps = False
    for kind, axes in plan:
        if kind in ("swap2", "agswap", "swap"):
            swaps = True
        if kind in ("ag", "a2a", "agswap") and axes not in groups:
            groups.append(axes)
    barrier = pltpu.get_barrier_semaphore()
    expected = 0
    for axes in groups:
        n = group_of(axes, sizes)
        me = my_index(axes, sizes)
        for d in range(1, n):
            peer = lax.rem(me + d, n)
            pl.semaphore_signal(
                barrier, inc=1, device_id=device_at(axes, peer, sizes), device_id_type=MESH
            )
            expected += 1
    if swaps:
        pl.semaphore_signal(barrier, inc=1, device_id=partner, device_id_type=MESH)
        expected += 1
    pl.semaphore_wait(barrier, expected)

    def remote(src, dst, send, recv, where):
        return pltpu.make_async_remote_copy(
            src_ref=src, dst_ref=dst, send_sem=send, recv_sem=recv, device_id=where,
            device_id_type=MESH,
        )

    pending = []
    forwards = []
    at = 0
    for slot, (kind, axes) in enumerate(plan):
        out = outs[slot]
        send, recv, local, fsend, frecv = sems[5 * slot : 5 * slot + 5]
        if kind == "swap2":
            first, second = ins[at], ins[at + 1]
            at += 2

            @pl.when(section == 0)
            def _():
                remote(second, out, send.at[0], recv.at[0], partner).start()

            @pl.when(section == 1)
            def _():
                remote(first, out, send.at[0], recv.at[0], partner).start()

            pending.append(remote(first, out, send.at[0], recv.at[0], partner))
            continue
        x = ins[at]
        at += 1
        if kind == "swap":
            copy = remote(x.at[1 - section], out, send.at[0], recv.at[0], partner)
            copy.start()
            pending.append(copy)
            continue
        n = group_of(axes, sizes)
        me = my_index(axes, sizes)
        target = out.at[section] if kind == "agswap" else out
        for d in range(1, n):
            peer = lax.rem(me + d, n)
            source = x.at[peer] if kind == "a2a" else x
            remote(
                source, target.at[me], send.at[peer], recv.at[me], device_at(axes, peer, sizes)
            ).start()
        own = pltpu.make_async_copy(x.at[me] if kind == "a2a" else x, target.at[me], local)
        own.start()
        if kind == "agswap":
            forward = remote(x, target.at[me], fsend.at[me], frecv.at[me], partner)
            forward.start()
        forwards.append((kind, axes, x, out, target, own, sems[5 * slot : 5 * slot + 5]))
    for kind, axes, x, out, target, own, (send, recv, local, fsend, frecv) in forwards:
        n = group_of(axes, sizes)
        me = my_index(axes, sizes)
        for d in range(1, n):
            peer = lax.rem(me + n - d, n)
            where = device_at(axes, peer, sizes)
            source = x.at[peer] if kind == "a2a" else x
            copy = remote(source, target.at[peer], send.at[peer], recv.at[peer], where)
            copy.wait_recv()
            if kind == "agswap":
                remote(
                    target.at[peer], target.at[peer], fsend.at[peer], frecv.at[peer], partner
                ).start()
        own.wait()
        for d in range(1, n):
            peer = lax.rem(me + n - d, n)
            where = device_at(axes, peer, sizes)
            source = x.at[peer] if kind == "a2a" else x
            remote(source, target.at[peer], send.at[peer], recv.at[peer], where).wait_send()
        if kind == "agswap":
            other = out.at[1 - section]
            for d in range(n):
                peer = lax.rem(me + n - d, n)
                copy = remote(
                    target.at[peer], other.at[peer], fsend.at[peer], frecv.at[peer], partner
                )
                copy.wait_send()
                copy.wait_recv()
    for copy in pending:
        copy.wait_send()
        copy.wait_recv()


def communicate(sizes, *ops):
    plan, arrays, shapes, scratch = [], [], [], []
    for kind, axes, x in ops:
        plan.append((kind, axes))
        if kind == "swap2":
            arrays.extend(x)
            n, shape, dtype = 1, x[0].shape, x[0].dtype
        else:
            arrays.append(x)
            n, shape, dtype = 1, x.shape, x.dtype
            if kind == "swap":
                shape = x.shape[1:]
            else:
                n = group_of(axes, sizes)
                if kind == "ag":
                    shape = (n,) + x.shape
                elif kind == "agswap":
                    shape = (2, n) + x.shape
        shapes.append(jax.ShapeDtypeStruct(shape, dtype))
        dma = pltpu.SemaphoreType.DMA
        scratch += [dma((n,)), dma((n,)), dma(()), dma((n,)), dma((n,))]
    key = (tuple(plan), tuple((a.shape, str(a.dtype)) for a in arrays))
    ident = IDS.setdefault(key, len(IDS))
    space = pl.BlockSpec(memory_space=pltpu.VMEM)
    out = pl.pallas_call(
        functools.partial(comm_kernel, tuple(plan), sizes, len(arrays)),
        out_shape=shapes,
        in_specs=[space] * len(arrays),
        out_specs=[space] * len(shapes),
        scratch_shapes=scratch,
        compiler_params=pltpu.CompilerParams(
            collective_id=ident, has_side_effects=True, vmem_limit_bytes=VMEM_LIMIT
        ),
        name="comm%d" % ident,
    )(*arrays)
    return out


def nt(a, b):
    return lax.dot_general(a, b, (((1,), (1,)), ((), ())), preferred_element_type=F32)


def tn(a, b):
    return lax.dot_general(a, b, (((0,), (0,)), ((), ())), preferred_element_type=F32)


def nn(a, b):
    return jnp.dot(a, b, preferred_element_type=F32)


def stack_heads(x, g):
    first = g * GROUP * HD
    return jnp.concatenate([x[:, first + i * HD : first + (i + 1) * HD] for i in range(GROUP)], 0)


def attend_kernel(chunk, q_ref, kv_ref, pos_ref, doc_ref, o_ref, lse_ref):
    rows = q_ref.shape[0]
    wide = GROUP * rows
    keys = kv_ref.shape[0]
    q = q_ref[...].astype(F32)
    pos = pos_ref[...]
    doc = doc_ref[...]
    for g in range(KV):
        qg = stack_heads(q, g).astype(BF)

        def step(i, carry, qg=qg, g=g):
            top, total, acc = carry
            base = pl.multiple_of(i * chunk, chunk)
            k = kv_ref[pl.ds(base, chunk), g * HD : (g + 1) * HD]
            v = kv_ref[pl.ds(base, chunk), KVW + g * HD : KVW + (g + 1) * HD]
            s = nt(k, qg) * 0.125
            at = base + lax.broadcasted_iota(jnp.int32, (chunk, wide), 0)
            s = jnp.where((at <= pos) & (at >= doc), s, FLOOR)
            new = jnp.maximum(top, jnp.max(s, 0, keepdims=True))
            scale = jnp.exp(top - new)
            p = jnp.exp(s - new)
            total = total * scale + jnp.sum(p, 0, keepdims=True)
            acc = acc * scale + tn(v, p.astype(BF))
            return new, total, acc

        top, total, acc = lax.fori_loop(
            0,
            keys // chunk,
            step,
            (
                jnp.full((1, wide), FLOOR, F32),
                jnp.zeros((1, wide), F32),
                jnp.zeros((HD, wide), F32),
            ),
        )
        out = jnp.transpose(acc / total)
        for i in range(GROUP):
            h = g * GROUP + i
            o_ref[:, h * HD : (h + 1) * HD] = out[i * rows : (i + 1) * rows, :].astype(BF)
        lse_ref[g : g + 1, :] = top + jnp.log(total)


def attend(q, kv, pos, doc):
    rows = q.shape[0]
    keys = kv.shape[0]
    return pl.pallas_call(
        functools.partial(attend_kernel, 512 if keys % 512 == 0 else keys),
        out_shape=[
            jax.ShapeDtypeStruct(q.shape, BF),
            jax.ShapeDtypeStruct((KV, GROUP * rows), F32),
        ],
        compiler_params=pltpu.CompilerParams(vmem_limit_bytes=VMEM_LIMIT),
        name="attend",
    )(q, kv, pos, doc)


def attend_back_kernel(
    chunk, q_ref, do_ref, o_ref, kv_ref, lse_ref, pos_ref, doc_ref, dq_ref, dkv_ref
):
    rows = q_ref.shape[0]
    wide = GROUP * rows
    keys = kv_ref.shape[0]
    q = q_ref[...].astype(F32)
    do = do_ref[...].astype(F32)
    prod = do * o_ref[...].astype(F32)
    pos = pos_ref[...]
    doc = doc_ref[...]
    for g in range(KV):
        qg = stack_heads(q, g).astype(BF)
        dog = stack_heads(do, g).astype(BF)
        delta = jnp.sum(jnp.transpose(stack_heads(prod, g)), 0, keepdims=True)
        lse = lse_ref[g : g + 1, :]

        def step(i, dq, qg=qg, dog=dog, delta=delta, lse=lse, g=g):
            base = pl.multiple_of(i * chunk, chunk)
            k = kv_ref[pl.ds(base, chunk), g * HD : (g + 1) * HD]
            v = kv_ref[pl.ds(base, chunk), KVW + g * HD : KVW + (g + 1) * HD]
            s = nt(k, qg) * 0.125
            at = base + lax.broadcasted_iota(jnp.int32, (chunk, wide), 0)
            s = jnp.where((at <= pos) & (at >= doc), s, FLOOR)
            p = jnp.exp(s - lse)
            dp = nt(v, dog)
            ds = (p * (dp - delta)).astype(BF)
            dkv_ref[pl.ds(base, chunk), g * HD : (g + 1) * HD] = (nn(ds, qg) * 0.125).astype(BF)
            dkv_ref[pl.ds(base, chunk), KVW + g * HD : KVW + (g + 1) * HD] = nn(
                p.astype(BF), dog
            ).astype(BF)
            return dq + tn(k, ds)

        dq = lax.fori_loop(0, keys // chunk, step, jnp.zeros((HD, wide), F32))
        out = jnp.transpose(dq * 0.125)
        for i in range(GROUP):
            h = g * GROUP + i
            dq_ref[:, h * HD : (h + 1) * HD] = out[i * rows : (i + 1) * rows, :]


def attend_back(q, do, o, kv, lse, pos, doc):
    keys = kv.shape[0]
    return pl.pallas_call(
        functools.partial(attend_back_kernel, 512 if keys % 512 == 0 else keys),
        out_shape=[jax.ShapeDtypeStruct(q.shape, F32), jax.ShapeDtypeStruct(kv.shape, BF)],
        compiler_params=pltpu.CompilerParams(vmem_limit_bytes=VMEM_LIMIT),
        name="attend_back",
    )(q, do, o, kv, lse, pos, doc)


def low_half(width):
    return (jnp.arange(width, dtype=jnp.int32) % HD < HD // 2)[None, :]


def rope(x, cos, sin):
    half = HD // 2
    w = x.shape[1]
    turned = jnp.where(low_half(w), -jnp.roll(x, -half, 1), jnp.roll(x, half, 1))
    return x * cos[:, :w] + turned * sin[:, :w]


def rope_back(x, cos, sin):
    half = HD // 2
    w = x.shape[1]
    scaled = x * sin[:, :w]
    turned = jnp.where(low_half(w), jnp.roll(scaled, -half, 1), -jnp.roll(scaled, half, 1))
    return x * cos[:, :w] + turned


def local(
    sizes, inputs, doc_start, attn_gain, w_q, w_k, w_v, w_o, mlp_gain, w_gate, w_up, w_down,
    cotangent,
):
    micro, rows, width = inputs.shape
    n_ctx, n_wt = sizes["ctx"], sizes["wt"]
    n_place = n_ctx * n_wt
    section = lax.axis_index("section")
    wt = lax.axis_index("wt")
    place = lax.axis_index("ctx") * n_wt + wt
    batch = n_place * rows
    keys = micro * batch
    qw = HEADS * HD
    fused = jnp.concatenate([w_q[0], w_k[0], w_v[0], w_o[0]], 1)
    x_in = lax.dynamic_index_in_dim(inputs, section, 0, keepdims=False)
    cot = lax.dynamic_index_in_dim(cotangent, section, 0, keepdims=False)
    gains = jnp.concatenate([attn_gain, mlp_gain], 0)
    weights, gates, ups, downs, all_gains, cot_rows = communicate(
        sizes,
        ("agswap", ("wt",), fused),
        ("ag", ("section",), w_gate[0]),
        ("ag", ("section",), w_up[0]),
        ("ag", ("section",), w_down[0]),
        ("ag", ("section",), gains),
        ("ag", ("wt",), cot.astype(BF)),
    )
    weights = weights.reshape(2, width, fused.shape[1])
    w_qkv = weights[:, :, : qw + 2 * KVW]
    w_out = weights[:, :, qw + 2 * KVW :]

    pos = section * batch + place * rows + jnp.arange(rows, dtype=jnp.int32)
    doc = lax.dynamic_slice(doc_start, (section, place * rows), (1, rows))[0]
    half = HD // 2
    inverse = 1.0 / THETA ** (jnp.arange(half).astype(F32) * 2.0 / HD)
    angles = (pos - doc).astype(F32)[:, None] * inverse[None, :]
    cos = jnp.tile(jnp.cos(angles), (1, 2 * HEADS))
    sin = jnp.tile(jnp.sin(angles), (1, 2 * HEADS))
    pos_row = jnp.tile(pos, GROUP)[None, :]
    doc_row = jnp.tile(doc, GROUP)[None, :]

    h_in = x_in
    saved = []
    for layer in range(2):
        ga, gm = all_gains[layer, 0], all_gains[layer, 1]
        h = h_in.astype(F32)
        r1 = lax.rsqrt(jnp.mean(h * h, -1, keepdims=True) + EPS)
        n1 = h * r1
        u = (n1 * ga).astype(BF)
        qkv = nn(u, w_qkv[layer])
        q = rope(qkv[:, :qw], cos, sin).astype(BF)
        k = rope(qkv[:, qw : qw + KVW], cos, sin).astype(BF)
        v = qkv[:, qw + KVW :].astype(BF)
        (kv,) = communicate(
            sizes, ("agswap", ("ctx", "wt"), jnp.concatenate([k, v], 1))
        )
        kv = kv.reshape(keys, 2 * KVW)
        o, lse = attend(q, kv, pos_row, doc_row)
        h2 = h + nn(o, w_out[layer])
        r2 = lax.rsqrt(jnp.mean(h2 * h2, -1, keepdims=True) + EPS)
        n2 = h2 * r2
        z = (n2 * gm).astype(BF)
        (zr,) = communicate(sizes, ("ag", ("wt",), z))
        zr = zr.reshape(n_wt * rows, width)
        g = nn(zr, gates[layer])
        up = nn(zr, ups[layer])
        act = (g * jax.nn.sigmoid(g) * up).astype(BF)
        branch = nn(act, downs[layer]).astype(BF).reshape(n_wt, rows, width)
        (parts,) = communicate(sizes, ("a2a", ("wt",), branch))
        out = (h2 + jnp.sum(parts.astype(F32), 0)).astype(BF)
        saved.append((n1, r1, u, q, kv, o, lse, n2, r2, zr, g, up, act))
        h_in = out
        if layer == 0:
            first_out = out
    second_out = h_in

    grads = [None, None]
    e = cot
    er = cot_rows.reshape(n_wt * rows, width)
    for layer in (1, 0):
        ga, gm = all_gains[layer, 0], all_gains[layer, 1]
        n1, r1, u, q, kv, o, lse, n2, r2, zr, g, up, act = saved[layer]
        if layer == 0:
            (er,) = communicate(sizes, ("ag", ("wt",), e))
            er = er.reshape(n_wt * rows, width)
            e = e.astype(F32)
        g_down = tn(act, er)
        da = nt(er, downs[layer])
        s = jax.nn.sigmoid(g)
        dg = (da * up * s * (1.0 + g * (1.0 - s))).astype(BF)
        du = (da * g * s).astype(BF)
        g_gate = tn(zr, dg)
        g_up = tn(zr, du)
        term = (nt(dg, gates[layer]) + nt(du, ups[layer])).astype(BF).reshape(n_wt, rows, width)
        (parts,) = communicate(sizes, ("a2a", ("wt",), term))
        dz = jnp.sum(parts.astype(F32), 0)
        g_gm = jnp.sum(dz * n2, 0)
        m2 = dz * gm
        dh2 = e + r2 * (m2 - n2 * jnp.mean(m2 * n2, -1, keepdims=True))
        ob = dh2.astype(BF)
        g_o = tn(o, ob)
        do = nt(ob, w_out[layer]).astype(BF)
        dq, dkv = attend_back(q, do, o, kv, lse, pos_row, doc_row)
        dkv = dkv.reshape(micro, n_place, rows, 2 * KVW)
        (theirs,) = communicate(sizes, ("swap", (), dkv))
        mine = lax.dynamic_index_in_dim(dkv, section, 0, keepdims=False)
        both = (mine.astype(F32) + theirs.astype(F32)).astype(BF)
        (pieces,) = communicate(sizes, ("a2a", ("ctx", "wt"), both))
        dkv_own = jnp.sum(pieces.astype(F32), 0)
        dqr = rope_back(dq, cos, sin).astype(BF)
        dkr = rope_back(dkv_own[:, :KVW], cos, sin).astype(BF)
        dvr = dkv_own[:, KVW:].astype(BF)
        dqkv = jnp.concatenate([dqr, dkr, dvr], 1)
        g_qkv = tn(u, dqkv)
        du_in = nt(dqkv, w_qkv[layer])
        g_ga = jnp.sum(du_in * n1, 0)
        m1 = du_in * ga
        e = (dh2 + r1 * (m1 - n1 * jnp.mean(m1 * n1, -1, keepdims=True))).astype(BF)
        grads[layer] = (
            jnp.concatenate([g_qkv, g_o], 1).astype(BF),
            g_gate.astype(BF),
            g_up.astype(BF),
            g_down.astype(BF),
            jnp.stack([g_ga, g_gm]),
        )
        if layer == 1:
            second_grad = e
    first_grad = e

    received = communicate(
        sizes,
        ("swap2", (), (first_out, second_out)),
        ("swap2", (), (first_grad, second_grad)),
        *[("swap2", (), pair) for pair in zip(grads[0], grads[1])],
    )

    def keep(pair):
        return jnp.where(section == 0, pair[0], pair[1])

    def whole(own, other):
        return jnp.where(section == 0, jnp.stack([own, other]), jnp.stack([other, own]))

    acts = whole(keep((first_out, second_out)), received[0])
    dacts = whole(keep((first_grad, second_grad)), received[1])
    summed = [
        keep(pair).astype(F32) + other.astype(F32)
        for pair, other in zip(zip(grads[0], grads[1]), received[2:])
    ]
    g_attn, g_gate, g_up, g_down, g_gain = summed
    cols = g_attn.shape[1]
    split = width // n_wt // n_ctx
    g_attn = (
        g_attn.astype(BF).reshape(n_wt, n_ctx, split, cols).transpose(1, 0, 2, 3)
    )
    hidden = g_gate.shape[1]
    r_attn, r_gate, r_up, r_down, r_gain = communicate(
        sizes,
        ("a2a", ("ctx",), g_attn),
        ("a2a", ("ctx",), g_gate.astype(BF).reshape(n_ctx, width // n_ctx, hidden)),
        ("a2a", ("ctx",), g_up.astype(BF).reshape(n_ctx, width // n_ctx, hidden)),
        ("a2a", ("ctx",), g_down.astype(BF).reshape(n_ctx, hidden // n_ctx, width)),
        ("ag", ("ctx", "wt"), g_gain),
    )

    def total(x):
        return jnp.sum(x.astype(F32), 0)

    (p_attn,) = communicate(sizes, ("a2a", ("wt",), total(r_attn).astype(BF)))
    f_attn, f_gate, f_up, f_down = communicate(
        sizes,
        ("ag", ("ctx",), total(p_attn).astype(BF)),
        ("ag", ("ctx",), total(r_gate).astype(BF)),
        ("ag", ("ctx",), total(r_up).astype(BF)),
        ("ag", ("ctx",), total(r_down).astype(BF)),
    )
    f_attn = f_attn.reshape(width // n_wt, cols).astype(F32)
    gain = lax.dynamic_slice_in_dim(total(r_gain), wt * (width // n_wt), width // n_wt, 1)
    return (
        acts[None],
        dacts[None],
        gain[0][None],
        f_attn[None, :, :qw],
        f_attn[None, :, qw : qw + KVW],
        f_attn[None, :, qw + KVW : qw + 2 * KVW],
        f_attn[None, :, qw + 2 * KVW :],
        gain[1][None],
        f_gate.reshape(1, width, hidden).astype(F32),
        f_up.reshape(1, width, hidden).astype(F32),
        f_down.reshape(1, hidden, width).astype(F32),
    )


def solution(mesh):
    in_specs = (
        P(None, ("ctx", "wt"), None),
        P(),
        P("section", None),
        P("section", "wt", None),
        P("section", "wt", None),
        P("section", "wt", None),
        P("section", "wt", None),
        P("section", None),
        P("section", None, "wt"),
        P("section", None, "wt"),
        P("section", "wt", None),
        P(None, ("ctx", "wt"), None),
    )
    out_specs = (
        P("section", None, ("ctx", "wt"), None),
        P("section", None, ("ctx", "wt"), None),
        P("section", "wt"),
        P("section", "wt", None),
        P("section", "wt", None),
        P("section", "wt", None),
        P("section", "wt", None),
        P("section", "wt"),
        P("section", None, "wt"),
        P("section", None, "wt"),
        P("section", "wt", None),
    )
    IDS.clear()
    sizes = dict(mesh.shape)
    return jax.shard_map(
        functools.partial(local, sizes), mesh=mesh, in_specs=in_specs, out_specs=out_specs,
        check_vma=False,
    )
```

```python
import functools

import jax
import jax.numpy as jnp
from jax import lax
from jax.experimental import pallas as pl
from jax.experimental.pallas import tpu as pltpu
from jax.sharding import PartitionSpec as P

HEADS = 9
KV = 3
GROUP = HEADS // KV
HD = 64
KVW = KV * HD
EPS = 1e-05
THETA = 100000.0
FLOOR = -1e30
BF = jnp.bfloat16
F32 = jnp.float32
VMEM_LIMIT = 60 * 1024 * 1024
MESH = pl.DeviceIdType.MESH

IDS = {}


def group_of(axes, sizes):
    count = 1
    for axis in axes:
        count *= sizes[axis]
    return count


def my_index(axes, sizes):
    index = 0
    for axis in axes:
        index = index * sizes[axis] + lax.axis_index(axis)
    return index


def device_at(axes, index, sizes):
    where = {}
    for axis in reversed(axes):
        where[axis] = lax.rem(index, sizes[axis])
        index = lax.div(index, sizes[axis])
    return where


def comm_kernel(plan, sizes, n_in, *refs):
    n_ops = len(plan)
    ins = refs[:n_in]
    outs = refs[n_in : n_in + n_ops]
    sems = refs[n_in + n_ops :]
    section = lax.axis_index("section")
    partner = {"section": 1 - section}
    n_wt, n_ctx = sizes["wt"], sizes["ctx"]
    w, c = lax.axis_index("wt"), lax.axis_index("ctx")
    left, right = {"wt": lax.rem(w + n_wt - 1, n_wt)}, {"wt": lax.rem(w + 1, n_wt)}
    has_left, has_right = w > 0, w < n_wt - 1
    groups, chain, swaps = [], False, False
    for kind, axes, only in plan:
        if kind in ("swap2", "swap", "to", "chainswap", "wide"):
            swaps = True
        if kind in ("chain", "chainswap", "wide"):
            chain = True
        if kind == "wide" and ("ctx",) not in groups:
            groups.append(("ctx",))
        if kind in ("ag", "a2a") and axes not in groups:
            groups.append(axes)
    if ("wt",) in groups:
        chain = False
    barrier = pltpu.get_barrier_semaphore()

    def greet(where):
        pl.semaphore_signal(barrier, inc=1, device_id=where, device_id_type=MESH)

    expected = 0
    for axes in groups:
        n = group_of(axes, sizes)
        me = my_index(axes, sizes)
        for d in range(1, n):
            greet(device_at(axes, lax.rem(me + d, n), sizes))
            expected += 1
    if swaps:
        greet(partner)
        expected += 1
    if chain:
        pl.when(has_left)(lambda: greet(left))
        pl.when(has_right)(lambda: greet(right))
        expected += lax.div(w + n_wt - 1, n_wt) + lax.div(2 * n_wt - 2 - w, n_wt)
    pl.semaphore_wait(barrier, expected)

    def remote(src, dst, send, recv, where):
        return pltpu.make_async_remote_copy(
            src_ref=src, dst_ref=dst, send_sem=send, recv_sem=recv, device_id=where,
            device_id_type=MESH,
        )

    second_phase = []
    last_phase = []

    def run(only, f):
        if only is None:
            f()
        else:
            pl.when(section == only)(lambda: (f(), None)[1])

    def simple(out, sem, slot_source):
        send, recv = sem[0], sem[1]
        copy = remote(slot_source, out, send.at[0], recv.at[0], partner)
        copy.start()
        return copy

    def start_group(kind, axes, x, out, sem):
        send, recv, local = sem[0], sem[1], sem[2]
        n = group_of(axes, sizes)
        me = my_index(axes, sizes)
        for d in range(1, n):
            peer = lax.rem(me + d, n)
            source = x.at[peer] if kind == "a2a" else x
            remote(
                source, out.at[me], send.at[peer], recv.at[me], device_at(axes, peer, sizes)
            ).start()
        pltpu.make_async_copy(x.at[me] if kind == "a2a" else x, out.at[me], local).start()

    def end_group(kind, axes, x, out, sem):
        send, recv, local = sem[0], sem[1], sem[2]
        n = group_of(axes, sizes)
        me = my_index(axes, sizes)
        for d in range(1, n):
            peer = lax.rem(me + n - d, n)
            where = device_at(axes, peer, sizes)
            source = x.at[peer] if kind == "a2a" else x
            copy = remote(source, out.at[peer], send.at[peer], recv.at[peer], where)
            copy.wait_recv()
            copy.wait_send()
        pltpu.make_async_copy(x.at[me] if kind == "a2a" else x, out.at[me], local).wait()

    at = 0
    for slot, (kind, axes, only) in enumerate(plan):
        out = outs[slot]
        sem = sems[6 * slot : 6 * slot + 6]
        send, recv, local, fsend, frecv, lsend = sem
        x = ins[at]
        at += 1
        if kind == "swap2":
            second = ins[at]
            at += 1
            run(0, functools.partial(simple, out, sem, second))
            run(1, functools.partial(simple, out, sem, x))

            def end(x=x, out=out, sem=sem):
                copy = remote(x, out, sem[0].at[0], sem[1].at[0], partner)
                copy.wait_send()
                copy.wait_recv()

            last_phase.append(end)
        elif kind == "swap":
            copy = simple(out, sem, x.at[1 - section])
            last_phase.append(lambda copy=copy: (copy.wait_send(), copy.wait_recv()))
        elif kind == "to":
            run(1 - only, functools.partial(simple, out, sem, x))
            copy = remote(x, out, send.at[0], recv.at[0], partner)
            last_phase.append(lambda copy=copy, only=only: run(1 - only, copy.wait_send))
            last_phase.append(lambda copy=copy, only=only: run(only, copy.wait_recv))
        elif kind in ("ag", "a2a"):
            run(only, functools.partial(start_group, kind, axes, x, out, sem))
            last_phase.append(
                functools.partial(
                    run, only, functools.partial(end_group, kind, axes, x, out, sem)
                )
            )
        else:
            swap = kind != "chain"
            wide = kind == "wide"
            mine = out.at[section] if swap else out
            column = mine.at[c] if wide else mine
            base = c * n_wt if wide else 0

            def spread(j, src, column=column, mine=mine, base=base, sem=sem, swap=swap, wide=wide):
                send, recv, local, fsend, frecv, lsend = sem
                if wide:
                    for d in range(1, n_ctx):
                        peer = lax.rem(c + d, n_ctx)
                        remote(
                            src, column.at[j], send.at[n_wt + peer * n_wt + j],
                            recv.at[base + j], {"ctx": peer},
                        ).start()
                if swap:
                    remote(src, column.at[j], fsend.at[base + j], frecv.at[base + j], partner).start()

            def hop(j, src, where, which, column=column, base=base, sem=sem):
                return remote(src, column.at[j], which, sem[1].at[base + j], where)

            pl.when(has_right)(lambda h=hop, x=x, send=send: h(w, x, right, send.at[w]).start())
            pl.when(has_left)(lambda h=hop, x=x, lsend=lsend: h(w, x, left, lsend).start())
            spread(w, x)
            pltpu.make_async_copy(x, column.at[w], local).start()
            second_phase.append((x, out, mine, column, base, sem, swap, wide, spread, hop))

    for t in range(1, n_wt):
        for x, out, mine, column, base, sem, swap, wide, spread, hop in second_phase:
            send, recv, local, fsend, frecv, lsend = sem

            @pl.when(w >= t)
            def _():
                j = w - t
                hop(j, x, left, send.at[j]).wait_recv()
                pl.when(has_right)(lambda: hop(j, column.at[j], right, send.at[j]).start())
                spread(j, column.at[j])

            @pl.when(w + t < n_wt)
            def _():
                j = w + t
                hop(j, x, right, send.at[j]).wait_recv()
                pl.when(has_left)(lambda: hop(j, column.at[j], left, send.at[j]).start())
                spread(j, column.at[j])

    for x, out, mine, column, base, sem, swap, wide, spread, hop in second_phase:
        send, recv, local, fsend, frecv, lsend = sem
        if wide:
            for d in range(1, n_ctx):
                peer = lax.rem(c + n_ctx - d, n_ctx)
                for j in range(n_wt):
                    k = peer * n_wt + j
                    got = mine.at[peer].at[j]
                    remote(x, got, send.at[n_wt + k], recv.at[k], {"ctx": peer}).wait_recv()
                    remote(got, got, fsend.at[k], frecv.at[k], partner).start()

    for end in last_phase:
        end()

    for x, out, mine, column, base, sem, swap, wide, spread, hop in second_phase:
        send, recv, local, fsend, frecv, lsend = sem
        pl.when(has_right)(lambda: hop(w, x, right, send.at[w]).wait_send())
        pl.when(has_left)(lambda: hop(w, x, left, lsend).wait_send())
        for t in range(1, n_wt):
            pl.when((w >= t) & has_right)(
                lambda: hop(w - t, x, right, send.at[w - t]).wait_send()
            )
            pl.when((w + t < n_wt) & has_left)(
                lambda: hop(w + t, x, left, send.at[w + t]).wait_send()
            )
        pltpu.make_async_copy(x, column.at[w], local).wait()
        if wide:
            for d in range(1, n_ctx):
                peer = lax.rem(c + d, n_ctx)
                for j in range(n_wt):
                    remote(
                        x, column.at[j], send.at[n_wt + peer * n_wt + j], recv.at[j],
                        {"ctx": peer},
                    ).wait_send()
        if swap:
            count = n_ctx * n_wt if wide else n_wt
            for k in range(count):
                here = mine.at[k // n_wt].at[k % n_wt] if wide else mine.at[k]
                copy = remote(here, here, fsend.at[k], frecv.at[k], partner)
                copy.wait_send()
                copy.wait_recv()


def communicate(sizes, *ops):
    plan, arrays, shapes, scratch = [], [], [], []
    n_wt, n_ctx = sizes["wt"], sizes["ctx"]
    for kind, axes, x, *only in ops:
        plan.append((kind, axes, only[0] if only else None))
        n = 1
        if kind == "swap2":
            arrays.extend(x)
            shape, dtype = x[0].shape, x[0].dtype
        else:
            arrays.append(x)
            shape, dtype = x.shape, x.dtype
            if kind == "swap":
                shape = x.shape[1:]
            elif kind == "a2a":
                n = group_of(axes, sizes)
            elif kind == "ag":
                n = group_of(axes, sizes)
                shape = (n,) + x.shape
            elif kind == "chain":
                n = n_wt
                shape = (n_wt,) + x.shape
            elif kind == "chainswap":
                n = n_wt
                shape = (2, n_wt) + x.shape
            elif kind == "wide":
                n = n_wt * (n_ctx + 1)
                shape = (2, n_ctx, n_wt) + x.shape
        shapes.append(jax.ShapeDtypeStruct(shape, dtype))
        dma = pltpu.SemaphoreType.DMA
        scratch += [dma((n,)), dma((n,)), dma(()), dma((n,)), dma((n,)), dma(())]
    key = (tuple(plan), tuple((a.shape, str(a.dtype)) for a in arrays))
    ident = IDS.setdefault(key, len(IDS))
    space = pl.BlockSpec(memory_space=pltpu.VMEM)
    out = pl.pallas_call(
        functools.partial(comm_kernel, tuple(plan), sizes, len(arrays)),
        out_shape=shapes,
        in_specs=[space] * len(arrays),
        out_specs=[space] * len(shapes),
        scratch_shapes=scratch,
        compiler_params=pltpu.CompilerParams(
            collective_id=ident, has_side_effects=True, vmem_limit_bytes=VMEM_LIMIT
        ),
        name="comm%d" % ident,
    )(*arrays)
    return out


def nt(a, b):
    return lax.dot_general(a, b, (((1,), (1,)), ((), ())), preferred_element_type=F32)


def tn(a, b):
    return lax.dot_general(a, b, (((0,), (0,)), ((), ())), preferred_element_type=F32)


def nn(a, b):
    return jnp.dot(a, b, preferred_element_type=F32)


def stack_heads(x, g):
    first = g * GROUP * HD
    return jnp.concatenate([x[:, first + i * HD : first + (i + 1) * HD] for i in range(GROUP)], 0)


def attend_kernel(chunk, q_ref, kv_ref, pos_ref, doc_ref, o_ref, lse_ref):
    rows = q_ref.shape[0]
    wide = GROUP * rows
    keys = kv_ref.shape[0]
    q = q_ref[...].astype(F32)
    pos = pos_ref[...]
    doc = doc_ref[...]
    for g in range(KV):
        qg = stack_heads(q, g).astype(BF)

        def step(i, carry, qg=qg, g=g):
            top, total, acc = carry
            base = pl.multiple_of(i * chunk, chunk)
            k = kv_ref[pl.ds(base, chunk), g * HD : (g + 1) * HD]
            v = kv_ref[pl.ds(base, chunk), KVW + g * HD : KVW + (g + 1) * HD]
            s = nt(k, qg) * 0.125
            at = base + lax.broadcasted_iota(jnp.int32, (chunk, wide), 0)
            s = jnp.where((at <= pos) & (at >= doc), s, FLOOR)
            new = jnp.maximum(top, jnp.max(s, 0, keepdims=True))
            scale = jnp.exp(top - new)
            p = jnp.exp(s - new)
            total = total * scale + jnp.sum(p, 0, keepdims=True)
            acc = acc * scale + tn(v, p.astype(BF))
            return new, total, acc

        top, total, acc = lax.fori_loop(
            0,
            keys // chunk,
            step,
            (
                jnp.full((1, wide), FLOOR, F32),
                jnp.zeros((1, wide), F32),
                jnp.zeros((HD, wide), F32),
            ),
        )
        out = jnp.transpose(acc / total)
        for i in range(GROUP):
            h = g * GROUP + i
            o_ref[:, h * HD : (h + 1) * HD] = out[i * rows : (i + 1) * rows, :].astype(BF)
        lse_ref[g : g + 1, :] = top + jnp.log(total)


def attend(q, kv, pos, doc):
    rows = q.shape[0]
    keys = kv.shape[0]
    return pl.pallas_call(
        functools.partial(attend_kernel, 512 if keys % 512 == 0 else keys),
        out_shape=[
            jax.ShapeDtypeStruct(q.shape, BF),
            jax.ShapeDtypeStruct((KV, GROUP * rows), F32),
        ],
        compiler_params=pltpu.CompilerParams(vmem_limit_bytes=VMEM_LIMIT),
        name="attend",
    )(q, kv, pos, doc)


def attend_back_kernel(
    chunk, q_ref, do_ref, o_ref, kv_ref, lse_ref, pos_ref, doc_ref, dq_ref, dkv_ref
):
    rows = q_ref.shape[0]
    wide = GROUP * rows
    keys = kv_ref.shape[0]
    q = q_ref[...].astype(F32)
    do = do_ref[...].astype(F32)
    prod = do * o_ref[...].astype(F32)
    pos = pos_ref[...]
    doc = doc_ref[...]
    for g in range(KV):
        qg = stack_heads(q, g).astype(BF)
        dog = stack_heads(do, g).astype(BF)
        delta = jnp.sum(jnp.transpose(stack_heads(prod, g)), 0, keepdims=True)
        lse = lse_ref[g : g + 1, :]

        def step(i, dq, qg=qg, dog=dog, delta=delta, lse=lse, g=g):
            base = pl.multiple_of(i * chunk, chunk)
            k = kv_ref[pl.ds(base, chunk), g * HD : (g + 1) * HD]
            v = kv_ref[pl.ds(base, chunk), KVW + g * HD : KVW + (g + 1) * HD]
            s = nt(k, qg) * 0.125
            at = base + lax.broadcasted_iota(jnp.int32, (chunk, wide), 0)
            s = jnp.where((at <= pos) & (at >= doc), s, FLOOR)
            p = jnp.exp(s - lse)
            dp = nt(v, dog)
            ds = (p * (dp - delta)).astype(BF)
            dkv_ref[pl.ds(base, chunk), g * HD : (g + 1) * HD] = (nn(ds, qg) * 0.125).astype(BF)
            dkv_ref[pl.ds(base, chunk), KVW + g * HD : KVW + (g + 1) * HD] = nn(
                p.astype(BF), dog
            ).astype(BF)
            return dq + tn(k, ds)

        dq = lax.fori_loop(0, keys // chunk, step, jnp.zeros((HD, wide), F32))
        out = jnp.transpose(dq * 0.125)
        for i in range(GROUP):
            h = g * GROUP + i
            dq_ref[:, h * HD : (h + 1) * HD] = out[i * rows : (i + 1) * rows, :]


def attend_back(q, do, o, kv, lse, pos, doc):
    keys = kv.shape[0]
    return pl.pallas_call(
        functools.partial(attend_back_kernel, 512 if keys % 512 == 0 else keys),
        out_shape=[jax.ShapeDtypeStruct(q.shape, F32), jax.ShapeDtypeStruct(kv.shape, BF)],
        compiler_params=pltpu.CompilerParams(vmem_limit_bytes=VMEM_LIMIT),
        name="attend_back",
    )(q, do, o, kv, lse, pos, doc)


def low_half(width):
    return (jnp.arange(width, dtype=jnp.int32) % HD < HD // 2)[None, :]


def rope(x, cos, sin):
    half = HD // 2
    w = x.shape[1]
    turned = jnp.where(low_half(w), -jnp.roll(x, -half, 1), jnp.roll(x, half, 1))
    return x * cos[:, :w] + turned * sin[:, :w]


def rope_back(x, cos, sin):
    half = HD // 2
    w = x.shape[1]
    scaled = x * sin[:, :w]
    turned = jnp.where(low_half(w), jnp.roll(scaled, -half, 1), -jnp.roll(scaled, half, 1))
    return x * cos[:, :w] + turned


def local(
    sizes, inputs, doc_start, attn_gain, w_q, w_k, w_v, w_o, mlp_gain, w_gate, w_up, w_down,
    cotangent,
):
    micro, rows, width = inputs.shape
    n_ctx, n_wt = sizes["ctx"], sizes["wt"]
    n_place = n_ctx * n_wt
    section = lax.axis_index("section")
    wt = lax.axis_index("wt")
    place = lax.axis_index("ctx") * n_wt + wt
    batch = n_place * rows
    keys = micro * batch
    qw = HEADS * HD
    fused = jnp.concatenate([w_q[0], w_k[0], w_v[0], w_o[0]], 1)
    x_in = lax.dynamic_index_in_dim(inputs, section, 0, keepdims=False)
    cot = lax.dynamic_index_in_dim(cotangent, section, 0, keepdims=False)
    gains = jnp.concatenate([attn_gain, mlp_gain], 0)
    weights, gates, ups, downs, all_gains, cot_rows = communicate(
        sizes,
        ("chainswap", (), fused),
        ("ag", ("section",), w_gate[0]),
        ("ag", ("section",), w_up[0]),
        ("ag", ("section",), w_down[0]),
        ("ag", ("section",), gains),
        ("chain", (), cot.astype(BF)),
    )
    weights = weights.reshape(2, width, fused.shape[1])
    w_qkv = weights[:, :, : qw + 2 * KVW]
    w_out = weights[:, :, qw + 2 * KVW :]

    pos = section * batch + place * rows + jnp.arange(rows, dtype=jnp.int32)
    doc = lax.dynamic_slice(doc_start, (section, place * rows), (1, rows))[0]
    half = HD // 2
    inverse = 1.0 / THETA ** (jnp.arange(half).astype(F32) * 2.0 / HD)
    angles = (pos - doc).astype(F32)[:, None] * inverse[None, :]
    cos = jnp.tile(jnp.cos(angles), (1, 2 * HEADS))
    sin = jnp.tile(jnp.sin(angles), (1, 2 * HEADS))
    pos_row = jnp.tile(pos, GROUP)[None, :]
    doc_row = jnp.tile(doc, GROUP)[None, :]

    h_in = x_in
    saved = []
    for layer in range(2):
        ga, gm = all_gains[layer, 0], all_gains[layer, 1]
        h = h_in.astype(F32)
        r1 = lax.rsqrt(jnp.mean(h * h, -1, keepdims=True) + EPS)
        n1 = h * r1
        u = (n1 * ga).astype(BF)
        qkv = nn(u, w_qkv[layer])
        q = rope(qkv[:, :qw], cos, sin).astype(BF)
        k = rope(qkv[:, qw : qw + KVW], cos, sin).astype(BF)
        v = qkv[:, qw + KVW :].astype(BF)
        (kv,) = communicate(
            sizes, ("wide", (), jnp.concatenate([k, v], 1))
        )
        kv = kv.reshape(keys, 2 * KVW)
        o, lse = attend(q, kv, pos_row, doc_row)
        h2 = h + nn(o, w_out[layer])
        r2 = lax.rsqrt(jnp.mean(h2 * h2, -1, keepdims=True) + EPS)
        n2 = h2 * r2
        z = (n2 * gm).astype(BF)
        (zr,) = communicate(sizes, ("chain", (), z))
        zr = zr.reshape(n_wt * rows, width)
        g = nn(zr, gates[layer])
        up = nn(zr, ups[layer])
        act = (g * jax.nn.sigmoid(g) * up).astype(BF)
        branch = nn(act, downs[layer]).astype(BF).reshape(n_wt, rows, width)
        saved.append((n1, r1, u, q, kv, o, lse, n2, r2, zr, g, up, act))
        if layer == 0:
            (parts,) = communicate(sizes, ("a2a", ("wt",), branch))
            h_in = first_out = (h2 + jnp.sum(parts.astype(F32), 0)).astype(BF)

    def total(x):
        return jnp.sum(x.astype(F32), 0)

    def summed(own, other):
        return (own.astype(F32) + other.astype(F32)).astype(BF)

    hidden = w_gate.shape[2]
    cols = fused.shape[1]
    ctx = ("ctx",)
    split = width // n_wt // n_ctx

    def mlp_chunks(parts):
        gate, lift, down = parts
        return (
            gate.reshape(n_ctx, width // n_ctx, hidden),
            lift.reshape(n_ctx, width // n_ctx, hidden),
            down.reshape(n_ctx, hidden // n_ctx, width),
        )

    def attn_chunks(x):
        return x.reshape(n_wt, n_ctx, split, cols).transpose(1, 0, 2, 3)

    def many(kind, axes, items, only):
        return [(kind, axes, item, only) for item in items]

    e = cot
    er = cot_rows.reshape(n_wt * rows, width)
    for layer in (1, 0):
        ga, gm = all_gains[layer, 0], all_gains[layer, 1]
        n1, r1, u, q, kv, o, lse, n2, r2, zr, g, up, act = saved[layer]
        if layer == 0:
            er, attn1_theirs, gain1_theirs, *mlp1 = communicate(
                sizes,
                ("chain", (), e),
                ("to", (), attn1, 1),
                ("to", (), gain1, 1),
                *many("a2a", ctx, mlp_chunks(mlp1), 1),
            )
            mlp1 = [total(item).astype(BF) for item in mlp1]
            attn1 = attn_chunks(summed(attn1, attn1_theirs))
            er = er.reshape(n_wt * rows, width)
            e = e.astype(F32)
        g_down = tn(act, er)
        da = nt(er, downs[layer])
        s = jax.nn.sigmoid(g)
        dg = (da * up * s * (1.0 + g * (1.0 - s))).astype(BF)
        du = (da * g * s).astype(BF)
        g_gate = tn(zr, dg)
        g_up = tn(zr, du)
        mlp = (g_gate.astype(BF), g_up.astype(BF), g_down.astype(BF))
        term = (nt(dg, gates[layer]) + nt(du, ups[layer])).astype(BF).reshape(n_wt, rows, width)
        if layer == 1:
            (parts,) = communicate(sizes, ("a2a", ("wt",), term))
        else:
            parts, attn1 = communicate(
                sizes, ("a2a", ("wt",), term), ("a2a", ctx, attn1, 1)
            )
            attn1 = total(attn1).astype(BF)
        dz = total(parts)
        g_gm = jnp.sum(dz * n2, 0)
        m2 = dz * gm
        dh2 = e + r2 * (m2 - n2 * jnp.mean(m2 * n2, -1, keepdims=True))
        ob = dh2.astype(BF)
        g_o = tn(o, ob)
        do = nt(ob, w_out[layer]).astype(BF)
        dq, dkv = attend_back(q, do, o, kv, lse, pos_row, doc_row)
        dkv = dkv.reshape(micro, n_place, rows, 2 * KVW)
        if layer == 1:
            theirs, *mlp1 = communicate(sizes, ("swap", (), dkv), *many("to", (), mlp, 1))
            mlp1 = [summed(own, other) for own, other in zip(mlp, mlp1)]
        else:
            theirs, parts, *rest = communicate(
                sizes,
                ("swap", (), dkv),
                ("a2a", ("wt",), branch),
                *many("to", (), mlp, 0),
                *many("ag", ctx, mlp1, 1),
            )
            mlp0 = mlp_chunks([summed(own, other) for own, other in zip(mlp, rest[:3])])
            mlp1 = rest[3:]
            second_out = (h2 + total(parts)).astype(BF)
        mine = lax.dynamic_index_in_dim(dkv, section, 0, keepdims=False)
        both = summed(mine, theirs)
        if layer == 1:
            (pieces,) = communicate(sizes, ("a2a", ("ctx", "wt"), both))
        else:
            pieces, attn1 = communicate(
                sizes, ("a2a", ("ctx", "wt"), both), ("a2a", ("wt",), attn1, 1)
            )
            attn1 = total(attn1).astype(BF)
        dkv_own = total(pieces)
        dqr = rope_back(dq, cos, sin).astype(BF)
        dkr = rope_back(dkv_own[:, :KVW], cos, sin).astype(BF)
        dvr = dkv_own[:, KVW:].astype(BF)
        dqkv = jnp.concatenate([dqr, dkr, dvr], 1)
        g_qkv = tn(u, dqkv)
        du_in = nt(dqkv, w_qkv[layer])
        g_ga = jnp.sum(du_in * n1, 0)
        m1 = du_in * ga
        e = (dh2 + r1 * (m1 - n1 * jnp.mean(m1 * n1, -1, keepdims=True))).astype(BF)
        attn = jnp.concatenate([g_qkv, g_o], 1).astype(BF)
        gain = jnp.stack([g_ga, g_gm])
        if layer == 1:
            second_grad, attn1, gain1 = e, attn, gain
    first_grad = e

    other_out, other_grad, attn0, gain0, attn1, *mlp0 = communicate(
        sizes,
        ("swap2", (), (first_out, second_out)),
        ("swap2", (), (first_grad, second_grad)),
        ("to", (), attn, 0),
        ("to", (), gain, 0),
        ("ag", ctx, attn1, 1),
        *many("a2a", ctx, mlp0, 0),
    )
    mlp0 = [total(item).astype(BF) for item in mlp0]
    gain = jnp.where(section == 0, gain + gain0, gain1 + gain1_theirs)
    attn0, gain = communicate(
        sizes,
        ("a2a", ctx, attn_chunks(summed(attn, attn0)), 0),
        ("ag", ("ctx", "wt"), gain),
    )
    attn0, *mlp0 = communicate(
        sizes, ("a2a", ("wt",), total(attn0).astype(BF), 0), *many("ag", ctx, mlp0, 0)
    )
    (attn0,) = communicate(sizes, ("ag", ctx, total(attn0).astype(BF), 0))

    def keep(first, second):
        return jnp.where(section == 0, first, second)

    def whole(first, second, other):
        return jnp.where(section == 0, jnp.stack([first, other]), jnp.stack([other, second]))

    acts = whole(first_out, second_out, other_out)
    dacts = whole(first_grad, second_grad, other_grad)
    f_attn = keep(attn0, attn1).reshape(width // n_wt, cols).astype(F32)
    f_gate, f_up, f_down = [keep(a, b).astype(F32) for a, b in zip(mlp0, mlp1)]
    gain = lax.dynamic_slice_in_dim(total(gain), wt * (width // n_wt), width // n_wt, 1)
    return (
        acts[None],
        dacts[None],
        gain[0][None],
        f_attn[None, :, :qw],
        f_attn[None, :, qw : qw + KVW],
        f_attn[None, :, qw + KVW : qw + 2 * KVW],
        f_attn[None, :, qw + 2 * KVW :],
        gain[1][None],
        f_gate.reshape(1, width, hidden),
        f_up.reshape(1, width, hidden),
        f_down.reshape(1, hidden, width),
    )


def solution(mesh):
    in_specs = (
        P(None, ("ctx", "wt"), None),
        P(),
        P("section", None),
        P("section", "wt", None),
        P("section", "wt", None),
        P("section", "wt", None),
        P("section", "wt", None),
        P("section", None),
        P("section", None, "wt"),
        P("section", None, "wt"),
        P("section", "wt", None),
        P(None, ("ctx", "wt"), None),
    )
    out_specs = (
        P("section", None, ("ctx", "wt"), None),
        P("section", None, ("ctx", "wt"), None),
        P("section", "wt"),
        P("section", "wt", None),
        P("section", "wt", None),
        P("section", "wt", None),
        P("section", "wt", None),
        P("section", "wt"),
        P("section", None, "wt"),
        P("section", None, "wt"),
        P("section", "wt", None),
    )
    IDS.clear()
    sizes = dict(mesh.shape)
    return jax.shard_map(
        functools.partial(local, sizes), mesh=mesh, in_specs=in_specs, out_specs=out_specs,
        check_vma=False,
    )
```

```python
import functools

import jax
import jax.numpy as jnp
from jax import lax
from jax.experimental import pallas as pl
from jax.experimental.pallas import tpu as pltpu
from jax.sharding import PartitionSpec as P

HEADS = 9
KV = 3
GROUP = HEADS // KV
HD = 64
KVW = KV * HD
EPS = 1e-05
THETA = 100000.0
FLOOR = -1e30
BF = jnp.bfloat16
F32 = jnp.float32
VMEM_LIMIT = 60 * 1024 * 1024
MESH = pl.DeviceIdType.MESH

IDS = {}


def group_of(axes, sizes):
    count = 1
    for axis in axes:
        count *= sizes[axis]
    return count


def my_index(axes, sizes):
    index = 0
    for axis in axes:
        index = index * sizes[axis] + lax.axis_index(axis)
    return index


def device_at(axes, index, sizes):
    where = {}
    for axis in reversed(axes):
        where[axis] = lax.rem(index, sizes[axis])
        index = lax.div(index, sizes[axis])
    return where


def comm_kernel(plan, sizes, n_in, *refs):
    n_ops = len(plan)
    ins = refs[:n_in]
    outs = refs[n_in : n_in + n_ops]
    sems = refs[n_in + n_ops :]
    section = lax.axis_index("section")
    partner = {"section": 1 - section}
    n_wt, n_ctx = sizes["wt"], sizes["ctx"]
    w, c = lax.axis_index("wt"), lax.axis_index("ctx")
    left, right = {"wt": lax.rem(w + n_wt - 1, n_wt)}, {"wt": lax.rem(w + 1, n_wt)}
    has_left, has_right = w > 0, w < n_wt - 1
    groups, chain, swaps = [], False, False
    for kind, axes, only in plan:
        if kind in ("swap2", "swap", "to", "chainswap", "wide"):
            swaps = True
        if kind in ("chain", "chainswap", "wide"):
            chain = True
        if kind == "wide" and ("ctx",) not in groups:
            groups.append(("ctx",))
        if kind in ("ag", "a2a") and axes not in groups:
            groups.append(axes)
    if ("wt",) in groups:
        chain = False
    barrier = pltpu.get_barrier_semaphore()

    def greet(where):
        pl.semaphore_signal(barrier, inc=1, device_id=where, device_id_type=MESH)

    expected = 0
    for axes in groups:
        n = group_of(axes, sizes)
        me = my_index(axes, sizes)
        for d in range(1, n):
            greet(device_at(axes, lax.rem(me + d, n), sizes))
            expected += 1
    if swaps:
        greet(partner)
        expected += 1
    if chain:
        pl.when(has_left)(lambda: greet(left))
        pl.when(has_right)(lambda: greet(right))
        expected += lax.div(w + n_wt - 1, n_wt) + lax.div(2 * n_wt - 2 - w, n_wt)
    pl.semaphore_wait(barrier, expected)

    def remote(src, dst, send, recv, where):
        return pltpu.make_async_remote_copy(
            src_ref=src, dst_ref=dst, send_sem=send, recv_sem=recv, device_id=where,
            device_id_type=MESH,
        )

    second_phase = []
    last_phase = []

    def run(only, f):
        if only is None:
            f()
        else:
            pl.when(section == only)(lambda: (f(), None)[1])

    def simple(out, sem, slot_source):
        send, recv = sem[0], sem[1]
        copy = remote(slot_source, out, send.at[0], recv.at[0], partner)
        copy.start()
        return copy

    def start_group(kind, axes, x, out, sem):
        send, recv, local = sem[0], sem[1], sem[2]
        n = group_of(axes, sizes)
        me = my_index(axes, sizes)
        for d in range(1, n):
            peer = lax.rem(me + d, n)
            source = x.at[peer] if kind == "a2a" else x
            remote(
                source, out.at[me], send.at[peer], recv.at[me], device_at(axes, peer, sizes)
            ).start()
        pltpu.make_async_copy(x.at[me] if kind == "a2a" else x, out.at[me], local).start()

    def end_group(kind, axes, x, out, sem):
        send, recv, local = sem[0], sem[1], sem[2]
        n = group_of(axes, sizes)
        me = my_index(axes, sizes)
        for d in range(1, n):
            peer = lax.rem(me + n - d, n)
            where = device_at(axes, peer, sizes)
            source = x.at[peer] if kind == "a2a" else x
            copy = remote(source, out.at[peer], send.at[peer], recv.at[peer], where)
            copy.wait_recv()
            copy.wait_send()
        pltpu.make_async_copy(x.at[me] if kind == "a2a" else x, out.at[me], local).wait()

    at = 0
    for slot, (kind, axes, only) in enumerate(plan):
        out = outs[slot]
        sem = sems[6 * slot : 6 * slot + 6]
        send, recv, local, fsend, frecv, lsend = sem
        x = ins[at]
        at += 1
        if kind == "swap2":
            second = ins[at]
            at += 1
            run(0, functools.partial(simple, out, sem, second))
            run(1, functools.partial(simple, out, sem, x))

            def end(x=x, out=out, sem=sem):
                copy = remote(x, out, sem[0].at[0], sem[1].at[0], partner)
                copy.wait_send()
                copy.wait_recv()

            last_phase.append(end)
        elif kind == "swap":
            copy = simple(out, sem, x.at[1 - section])
            last_phase.append(lambda copy=copy: (copy.wait_send(), copy.wait_recv()))
        elif kind == "to":
            run(1 - only, functools.partial(simple, out, sem, x))
            copy = remote(x, out, send.at[0], recv.at[0], partner)
            last_phase.append(lambda copy=copy, only=only: run(1 - only, copy.wait_send))
            last_phase.append(lambda copy=copy, only=only: run(only, copy.wait_recv))
        elif kind in ("ag", "a2a"):
            run(only, functools.partial(start_group, kind, axes, x, out, sem))
            last_phase.append(
                functools.partial(
                    run, only, functools.partial(end_group, kind, axes, x, out, sem)
                )
            )
        else:
            swap = kind != "chain"
            wide = kind == "wide"
            mine = out.at[section] if swap else out
            column = mine.at[c] if wide else mine
            base = c * n_wt if wide else 0

            def spread(j, src, column=column, mine=mine, base=base, sem=sem, swap=swap, wide=wide):
                send, recv, local, fsend, frecv, lsend = sem
                if wide:
                    for d in range(1, n_ctx):
                        peer = lax.rem(c + d, n_ctx)
                        remote(
                            src, column.at[j], send.at[n_wt + peer * n_wt + j],
                            recv.at[base + j], {"ctx": peer},
                        ).start()
                if swap:
                    remote(src, column.at[j], fsend.at[base + j], frecv.at[base + j], partner).start()

            def hop(j, src, where, which, column=column, base=base, sem=sem):
                return remote(src, column.at[j], which, sem[1].at[base + j], where)

            pl.when(has_right)(lambda h=hop, x=x, send=send: h(w, x, right, send.at[w]).start())
            pl.when(has_left)(lambda h=hop, x=x, lsend=lsend: h(w, x, left, lsend).start())
            spread(w, x)
            pltpu.make_async_copy(x, column.at[w], local).start()
            second_phase.append((x, out, mine, column, base, sem, swap, wide, spread, hop))

    for t in range(1, n_wt):
        for x, out, mine, column, base, sem, swap, wide, spread, hop in second_phase:
            send, recv, local, fsend, frecv, lsend = sem

            @pl.when(w >= t)
            def _():
                j = w - t
                hop(j, x, left, send.at[j]).wait_recv()
                pl.when(has_right)(lambda: hop(j, column.at[j], right, send.at[j]).start())
                spread(j, column.at[j])

            @pl.when(w + t < n_wt)
            def _():
                j = w + t
                hop(j, x, right, send.at[j]).wait_recv()
                pl.when(has_left)(lambda: hop(j, column.at[j], left, send.at[j]).start())
                spread(j, column.at[j])

    for x, out, mine, column, base, sem, swap, wide, spread, hop in second_phase:
        send, recv, local, fsend, frecv, lsend = sem
        if wide:
            for d in range(1, n_ctx):
                peer = lax.rem(c + n_ctx - d, n_ctx)
                for j in range(n_wt):
                    k = peer * n_wt + j
                    got = mine.at[peer].at[j]
                    remote(x, got, send.at[n_wt + k], recv.at[k], {"ctx": peer}).wait_recv()
                    remote(got, got, fsend.at[k], frecv.at[k], partner).start()

    for end in last_phase:
        end()

    for x, out, mine, column, base, sem, swap, wide, spread, hop in second_phase:
        send, recv, local, fsend, frecv, lsend = sem
        pl.when(has_right)(lambda: hop(w, x, right, send.at[w]).wait_send())
        pl.when(has_left)(lambda: hop(w, x, left, lsend).wait_send())
        for t in range(1, n_wt):
            pl.when((w >= t) & has_right)(
                lambda: hop(w - t, x, right, send.at[w - t]).wait_send()
            )
            pl.when((w + t < n_wt) & has_left)(
                lambda: hop(w + t, x, left, send.at[w + t]).wait_send()
            )
        pltpu.make_async_copy(x, column.at[w], local).wait()
        if wide:
            for d in range(1, n_ctx):
                peer = lax.rem(c + d, n_ctx)
                for j in range(n_wt):
                    remote(
                        x, column.at[j], send.at[n_wt + peer * n_wt + j], recv.at[j],
                        {"ctx": peer},
                    ).wait_send()
        if swap:
            count = n_ctx * n_wt if wide else n_wt
            for k in range(count):
                here = mine.at[k // n_wt].at[k % n_wt] if wide else mine.at[k]
                copy = remote(here, here, fsend.at[k], frecv.at[k], partner)
                copy.wait_send()
                copy.wait_recv()


def communicate(sizes, *ops):
    plan, arrays, shapes, scratch = [], [], [], []
    n_wt, n_ctx = sizes["wt"], sizes["ctx"]
    for kind, axes, x, *only in ops:
        plan.append((kind, axes, only[0] if only else None))
        n = 1
        if kind == "swap2":
            arrays.extend(x)
            shape, dtype = x[0].shape, x[0].dtype
        else:
            arrays.append(x)
            shape, dtype = x.shape, x.dtype
            if kind == "swap":
                shape = x.shape[1:]
            elif kind == "a2a":
                n = group_of(axes, sizes)
            elif kind == "ag":
                n = group_of(axes, sizes)
                shape = (n,) + x.shape
            elif kind == "chain":
                n = n_wt
                shape = (n_wt,) + x.shape
            elif kind == "chainswap":
                n = n_wt
                shape = (2, n_wt) + x.shape
            elif kind == "wide":
                n = n_wt * (n_ctx + 1)
                shape = (2, n_ctx, n_wt) + x.shape
        shapes.append(jax.ShapeDtypeStruct(shape, dtype))
        dma = pltpu.SemaphoreType.DMA
        scratch += [dma((n,)), dma((n,)), dma(()), dma((n,)), dma((n,)), dma(())]
    key = (tuple(plan), tuple((a.shape, str(a.dtype)) for a in arrays))
    ident = IDS.setdefault(key, len(IDS))
    space = pl.BlockSpec(memory_space=pltpu.VMEM)
    out = pl.pallas_call(
        functools.partial(comm_kernel, tuple(plan), sizes, len(arrays)),
        out_shape=shapes,
        in_specs=[space] * len(arrays),
        out_specs=[space] * len(shapes),
        scratch_shapes=scratch,
        compiler_params=pltpu.CompilerParams(
            collective_id=ident, has_side_effects=True, vmem_limit_bytes=VMEM_LIMIT
        ),
        name="comm%d" % ident,
    )(*arrays)
    return out


def nt(a, b):
    return lax.dot_general(a, b, (((1,), (1,)), ((), ())), preferred_element_type=F32)


def tn(a, b):
    return lax.dot_general(a, b, (((0,), (0,)), ((), ())), preferred_element_type=F32)


def nn(a, b):
    return jnp.dot(a, b, preferred_element_type=F32)


def stack_heads(x, g):
    first = g * GROUP * HD
    return jnp.concatenate([x[:, first + i * HD : first + (i + 1) * HD] for i in range(GROUP)], 0)


def attend_kernel(chunk, q_ref, kv_ref, pos_ref, doc_ref, o_ref, lse_ref):
    rows = q_ref.shape[0]
    wide = GROUP * rows
    keys = kv_ref.shape[0]
    q = q_ref[...].astype(F32)
    pos = pos_ref[...]
    doc = doc_ref[...]
    for g in range(KV):
        qg = stack_heads(q, g).astype(BF)

        def step(i, carry, qg=qg, g=g):
            top, total, acc = carry
            base = pl.multiple_of(i * chunk, chunk)
            k = kv_ref[pl.ds(base, chunk), g * HD : (g + 1) * HD]
            v = kv_ref[pl.ds(base, chunk), KVW + g * HD : KVW + (g + 1) * HD]
            s = nt(k, qg) * 0.125
            at = base + lax.broadcasted_iota(jnp.int32, (chunk, wide), 0)
            s = jnp.where((at <= pos) & (at >= doc), s, FLOOR)
            new = jnp.maximum(top, jnp.max(s, 0, keepdims=True))
            scale = jnp.exp(top - new)
            p = jnp.exp(s - new)
            total = total * scale + jnp.sum(p, 0, keepdims=True)
            acc = acc * scale + tn(v, p.astype(BF))
            return new, total, acc

        top, total, acc = lax.fori_loop(
            0,
            keys // chunk,
            step,
            (
                jnp.full((1, wide), FLOOR, F32),
                jnp.zeros((1, wide), F32),
                jnp.zeros((HD, wide), F32),
            ),
        )
        out = jnp.transpose(acc / total)
        for i in range(GROUP):
            h = g * GROUP + i
            o_ref[:, h * HD : (h + 1) * HD] = out[i * rows : (i + 1) * rows, :].astype(BF)
        lse_ref[g : g + 1, :] = top + jnp.log(total)


def attend(q, kv, pos, doc):
    rows = q.shape[0]
    keys = kv.shape[0]
    return pl.pallas_call(
        functools.partial(attend_kernel, 512 if keys % 512 == 0 else keys),
        out_shape=[
            jax.ShapeDtypeStruct(q.shape, BF),
            jax.ShapeDtypeStruct((KV, GROUP * rows), F32),
        ],
        compiler_params=pltpu.CompilerParams(vmem_limit_bytes=VMEM_LIMIT),
        name="attend",
    )(q, kv, pos, doc)


def attend_back_kernel(
    chunk, q_ref, do_ref, o_ref, kv_ref, lse_ref, pos_ref, doc_ref, dq_ref, dkv_ref
):
    rows = q_ref.shape[0]
    wide = GROUP * rows
    keys = kv_ref.shape[0]
    q = q_ref[...].astype(F32)
    do = do_ref[...].astype(F32)
    prod = do * o_ref[...].astype(F32)
    pos = pos_ref[...]
    doc = doc_ref[...]
    for g in range(KV):
        qg = stack_heads(q, g).astype(BF)
        dog = stack_heads(do, g).astype(BF)
        delta = jnp.sum(jnp.transpose(stack_heads(prod, g)), 0, keepdims=True)
        lse = lse_ref[g : g + 1, :]

        def step(i, dq, qg=qg, dog=dog, delta=delta, lse=lse, g=g):
            base = pl.multiple_of(i * chunk, chunk)
            k = kv_ref[pl.ds(base, chunk), g * HD : (g + 1) * HD]
            v = kv_ref[pl.ds(base, chunk), KVW + g * HD : KVW + (g + 1) * HD]
            s = nt(k, qg) * 0.125
            at = base + lax.broadcasted_iota(jnp.int32, (chunk, wide), 0)
            s = jnp.where((at <= pos) & (at >= doc), s, FLOOR)
            p = jnp.exp(s - lse)
            dp = nt(v, dog)
            ds = (p * (dp - delta)).astype(BF)
            dkv_ref[pl.ds(base, chunk), g * HD : (g + 1) * HD] = (nn(ds, qg) * 0.125).astype(BF)
            dkv_ref[pl.ds(base, chunk), KVW + g * HD : KVW + (g + 1) * HD] = nn(
                p.astype(BF), dog
            ).astype(BF)
            return dq + tn(k, ds)

        dq = lax.fori_loop(0, keys // chunk, step, jnp.zeros((HD, wide), F32))
        out = jnp.transpose(dq * 0.125)
        for i in range(GROUP):
            h = g * GROUP + i
            dq_ref[:, h * HD : (h + 1) * HD] = out[i * rows : (i + 1) * rows, :]


def attend_back(q, do, o, kv, lse, pos, doc):
    keys = kv.shape[0]
    return pl.pallas_call(
        functools.partial(attend_back_kernel, 512 if keys % 512 == 0 else keys),
        out_shape=[jax.ShapeDtypeStruct(q.shape, F32), jax.ShapeDtypeStruct(kv.shape, BF)],
        compiler_params=pltpu.CompilerParams(vmem_limit_bytes=VMEM_LIMIT),
        name="attend_back",
    )(q, do, o, kv, lse, pos, doc)


def low_half(width):
    return (jnp.arange(width, dtype=jnp.int32) % HD < HD // 2)[None, :]


def rope(x, cos, sin):
    half = HD // 2
    w = x.shape[1]
    turned = jnp.where(low_half(w), -jnp.roll(x, -half, 1), jnp.roll(x, half, 1))
    return x * cos[:, :w] + turned * sin[:, :w]


def rope_back(x, cos, sin):
    half = HD // 2
    w = x.shape[1]
    scaled = x * sin[:, :w]
    turned = jnp.where(low_half(w), jnp.roll(scaled, -half, 1), -jnp.roll(scaled, half, 1))
    return x * cos[:, :w] + turned


def local(
    sizes, inputs, doc_start, attn_gain, w_q, w_k, w_v, w_o, mlp_gain, w_gate, w_up, w_down,
    cotangent,
):
    micro, rows, width = inputs.shape
    n_ctx, n_wt = sizes["ctx"], sizes["wt"]
    n_place = n_ctx * n_wt
    section = lax.axis_index("section")
    wt = lax.axis_index("wt")
    place = lax.axis_index("ctx") * n_wt + wt
    batch = n_place * rows
    keys = micro * batch
    qw = HEADS * HD
    fused = jnp.concatenate([w_q[0], w_k[0], w_v[0], w_o[0]], 1)
    x_in = lax.dynamic_index_in_dim(inputs, section, 0, keepdims=False)
    cot = lax.dynamic_index_in_dim(cotangent, section, 0, keepdims=False)
    gains = jnp.concatenate([attn_gain, mlp_gain], 0)
    weights, gates, ups, downs, all_gains, cot_rows = communicate(
        sizes,
        ("chainswap", (), fused),
        ("ag", ("section",), w_gate[0]),
        ("ag", ("section",), w_up[0]),
        ("ag", ("section",), w_down[0]),
        ("ag", ("section",), gains),
        ("chain", (), cot.astype(BF)),
    )
    weights = weights.reshape(2, width, fused.shape[1])
    w_qkv = weights[:, :, : qw + 2 * KVW]
    w_out = weights[:, :, qw + 2 * KVW :]

    pos = section * batch + place * rows + jnp.arange(rows, dtype=jnp.int32)
    doc = lax.dynamic_slice(doc_start, (section, place * rows), (1, rows))[0]
    half = HD // 2
    inverse = 1.0 / THETA ** (jnp.arange(half).astype(F32) * 2.0 / HD)
    angles = (pos - doc).astype(F32)[:, None] * inverse[None, :]
    cos = jnp.tile(jnp.cos(angles), (1, 2 * HEADS))
    sin = jnp.tile(jnp.sin(angles), (1, 2 * HEADS))
    pos_row = jnp.tile(pos, GROUP)[None, :]
    doc_row = jnp.tile(doc, GROUP)[None, :]

    h_in = x_in
    saved = []
    for layer in range(2):
        ga, gm = all_gains[layer, 0], all_gains[layer, 1]
        h = h_in.astype(F32)
        r1 = lax.rsqrt(jnp.mean(h * h, -1, keepdims=True) + EPS)
        n1 = h * r1
        u = (n1 * ga).astype(BF)
        qkv = nn(u, w_qkv[layer])
        q = rope(qkv[:, :qw], cos, sin).astype(BF)
        k = rope(qkv[:, qw : qw + KVW], cos, sin).astype(BF)
        v = qkv[:, qw + KVW :].astype(BF)
        (kv,) = communicate(
            sizes, ("wide", (), jnp.concatenate([k, v], 1))
        )
        kv = kv.reshape(keys, 2 * KVW)
        o, lse = attend(q, kv, pos_row, doc_row)
        h2 = h + nn(o, w_out[layer])
        r2 = lax.rsqrt(jnp.mean(h2 * h2, -1, keepdims=True) + EPS)
        n2 = h2 * r2
        z = (n2 * gm).astype(BF)
        (zr,) = communicate(sizes, ("ag", ("wt",), z))
        zr = zr.reshape(n_wt * rows, width)
        g = nn(zr, gates[layer])
        up = nn(zr, ups[layer])
        act = (g * jax.nn.sigmoid(g) * up).astype(BF)
        branch = nn(act, downs[layer]).astype(BF).reshape(n_wt, rows, width)
        saved.append((n1, r1, u, q, kv, o, lse, n2, r2, zr, g, up, act))
        if layer == 0:
            (parts,) = communicate(sizes, ("a2a", ("wt",), branch))
            h_in = first_out = (h2 + jnp.sum(parts.astype(F32), 0)).astype(BF)

    def total(x):
        return jnp.sum(x.astype(F32), 0)

    def summed(own, other):
        return (own.astype(F32) + other.astype(F32)).astype(BF)

    hidden = w_gate.shape[2]
    cols = fused.shape[1]
    ctx = ("ctx",)
    split = width // n_wt // n_ctx

    def mlp_chunks(parts):
        gate, lift, down = parts
        return (
            gate.reshape(n_ctx, width // n_ctx, hidden),
            lift.reshape(n_ctx, width // n_ctx, hidden),
            down.reshape(n_ctx, hidden // n_ctx, width),
        )

    def attn_chunks(x):
        return x.reshape(n_wt, n_ctx, split, cols).transpose(1, 0, 2, 3)

    def many(kind, axes, items, only):
        return [(kind, axes, item, only) for item in items]

    e = cot
    er = cot_rows.reshape(n_wt * rows, width)
    for layer in (1, 0):
        ga, gm = all_gains[layer, 0], all_gains[layer, 1]
        n1, r1, u, q, kv, o, lse, n2, r2, zr, g, up, act = saved[layer]
        if layer == 0:
            er, attn1_theirs, gain1_theirs, *mlp1 = communicate(
                sizes,
                ("ag", ("wt",), e),
                ("to", (), attn1, 1),
                ("to", (), gain1, 1),
                *many("a2a", ctx, mlp_chunks(mlp1), 1),
            )
            mlp1 = [total(item).astype(BF) for item in mlp1]
            attn1 = attn_chunks(summed(attn1, attn1_theirs))
            er = er.reshape(n_wt * rows, width)
            e = e.astype(F32)
        g_down = tn(act, er)
        da = nt(er, downs[layer])
        s = jax.nn.sigmoid(g)
        dg = (da * up * s * (1.0 + g * (1.0 - s))).astype(BF)
        du = (da * g * s).astype(BF)
        g_gate = tn(zr, dg)
        g_up = tn(zr, du)
        mlp = (g_gate.astype(BF), g_up.astype(BF), g_down.astype(BF))
        term = (nt(dg, gates[layer]) + nt(du, ups[layer])).astype(BF).reshape(n_wt, rows, width)
        if layer == 1:
            (parts,) = communicate(sizes, ("a2a", ("wt",), term))
        else:
            parts, attn1 = communicate(
                sizes, ("a2a", ("wt",), term), ("a2a", ctx, attn1, 1)
            )
            attn1 = total(attn1).astype(BF)
        dz = total(parts)
        g_gm = jnp.sum(dz * n2, 0)
        m2 = dz * gm
        dh2 = e + r2 * (m2 - n2 * jnp.mean(m2 * n2, -1, keepdims=True))
        ob = dh2.astype(BF)
        g_o = tn(o, ob)
        do = nt(ob, w_out[layer]).astype(BF)
        dq, dkv = attend_back(q, do, o, kv, lse, pos_row, doc_row)
        dkv = dkv.reshape(micro, n_place, rows, 2 * KVW)
        if layer == 1:
            theirs, *mlp1 = communicate(sizes, ("swap", (), dkv), *many("to", (), mlp, 1))
            mlp1 = [summed(own, other) for own, other in zip(mlp, mlp1)]
        else:
            theirs, parts, *rest = communicate(
                sizes,
                ("swap", (), dkv),
                ("a2a", ("wt",), branch),
                *many("to", (), mlp, 0),
                *many("ag", ctx, mlp1, 1),
            )
            mlp0 = mlp_chunks([summed(own, other) for own, other in zip(mlp, rest[:3])])
            mlp1 = rest[3:]
            second_out = (h2 + total(parts)).astype(BF)
        mine = lax.dynamic_index_in_dim(dkv, section, 0, keepdims=False)
        both = summed(mine, theirs)
        if layer == 1:
            (pieces,) = communicate(sizes, ("a2a", ("ctx", "wt"), both))
        else:
            pieces, attn1 = communicate(
                sizes, ("a2a", ("ctx", "wt"), both), ("a2a", ("wt",), attn1, 1)
            )
            attn1 = total(attn1).astype(BF)
        dkv_own = total(pieces)
        dqr = rope_back(dq, cos, sin).astype(BF)
        dkr = rope_back(dkv_own[:, :KVW], cos, sin).astype(BF)
        dvr = dkv_own[:, KVW:].astype(BF)
        dqkv = jnp.concatenate([dqr, dkr, dvr], 1)
        g_qkv = tn(u, dqkv)
        du_in = nt(dqkv, w_qkv[layer])
        g_ga = jnp.sum(du_in * n1, 0)
        m1 = du_in * ga
        e = (dh2 + r1 * (m1 - n1 * jnp.mean(m1 * n1, -1, keepdims=True))).astype(BF)
        attn = jnp.concatenate([g_qkv, g_o], 1).astype(BF)
        gain = jnp.stack([g_ga, g_gm])
        if layer == 1:
            second_grad, attn1, gain1 = e, attn, gain
    first_grad = e

    other_out, other_grad, attn0, gain0, attn1, *mlp0 = communicate(
        sizes,
        ("swap2", (), (first_out, second_out)),
        ("swap2", (), (first_grad, second_grad)),
        ("to", (), attn, 0),
        ("to", (), gain, 0),
        ("ag", ctx, attn1, 1),
        *many("a2a", ctx, mlp0, 0),
    )
    mlp0 = [total(item).astype(BF) for item in mlp0]
    gain = jnp.where(section == 0, gain + gain0, gain1 + gain1_theirs)
    attn0, gain = communicate(
        sizes,
        ("a2a", ctx, attn_chunks(summed(attn, attn0)), 0),
        ("ag", ("ctx", "wt"), gain),
    )
    attn0, *mlp0 = communicate(
        sizes, ("a2a", ("wt",), total(attn0).astype(BF), 0), *many("ag", ctx, mlp0, 0)
    )
    (attn0,) = communicate(sizes, ("ag", ctx, total(attn0).astype(BF), 0))

    def keep(first, second):
        return jnp.where(section == 0, first, second)

    def whole(first, second, other):
        return jnp.where(section == 0, jnp.stack([first, other]), jnp.stack([other, second]))

    acts = whole(first_out, second_out, other_out)
    dacts = whole(first_grad, second_grad, other_grad)
    f_attn = keep(attn0, attn1).reshape(width // n_wt, cols).astype(F32)
    f_gate, f_up, f_down = [keep(a, b).astype(F32) for a, b in zip(mlp0, mlp1)]
    gain = lax.dynamic_slice_in_dim(total(gain), wt * (width // n_wt), width // n_wt, 1)
    return (
        acts[None],
        dacts[None],
        gain[0][None],
        f_attn[None, :, :qw],
        f_attn[None, :, qw : qw + KVW],
        f_attn[None, :, qw + KVW : qw + 2 * KVW],
        f_attn[None, :, qw + 2 * KVW :],
        gain[1][None],
        f_gate.reshape(1, width, hidden),
        f_up.reshape(1, width, hidden),
        f_down.reshape(1, hidden, width),
    )


def solution(mesh):
    in_specs = (
        P(None, ("ctx", "wt"), None),
        P(),
        P("section", None),
        P("section", "wt", None),
        P("section", "wt", None),
        P("section", "wt", None),
        P("section", "wt", None),
        P("section", None),
        P("section", None, "wt"),
        P("section", None, "wt"),
        P("section", "wt", None),
        P(None, ("ctx", "wt"), None),
    )
    out_specs = (
        P("section", None, ("ctx", "wt"), None),
        P("section", None, ("ctx", "wt"), None),
        P("section", "wt"),
        P("section", "wt", None),
        P("section", "wt", None),
        P("section", "wt", None),
        P("section", "wt", None),
        P("section", "wt"),
        P("section", None, "wt"),
        P("section", None, "wt"),
        P("section", "wt", None),
    )
    IDS.clear()
    sizes = dict(mesh.shape)
    return jax.shard_map(
        functools.partial(local, sizes), mesh=mesh, in_specs=in_specs, out_specs=out_specs,
        check_vma=False,
    )
```
